32 devices in a mesh: beam: 2 (over y), freq: 8 (over z, x), tm: 2 (over core).
Axes of the slice: x: 2, y: 2, z: 4, core: 2. Of those that a mesh axis runs over, the one named last changes fastest.
Arguments:
- voltages: bfloat16 [4, 8192, 1024], P('beam', 'tm', 'freq'), parts along dimension 0, may hold values from -6 to 6
- pfb_taps: float32 [16, 128], replicated, may hold values from -1.5 to 1.5
- local_shift: int32 [7, 512], P(None, 'freq'), may hold values from 0 to 7
- cross_shift: int32 [3, 64], P(None, 'freq'), may hold values from 0 to 31, as said below
- tap_index: int32 [32, 128], replicated, may hold values from 0 to 255
- tap_weight: float32 [32, 128], replicated, may hold values from -0.5 to 0.5
Outputs:
- dedispersed: float32 [128, 8192], P(('beam', 'freq'), 'tm'), parts along dimension 0
- scores: float32 [128, 32, 256], P(('beam', 'freq'), None, 'tm'), parts along dimension 0
The draws below stay inside these ranges and needn't reach their ends.
There are 2 independent parts, one for each index of `beam`. The reference program is written for one: setup_inputs(seed, part) draws one part's arguments, and reference() takes and returns one part's arrays. A program takes and returns all parts, laid end to end along the dimension named above; an argument that names none is the same for every part. Nothing has to cross between parts.
Inputs may be any that keep to these rules, and one draw needn't show every extreme that they name: `cross_shift`: row j holds values 0 to 8 * 2**j - 1, and reaches that value.
All inputs are finite; a program needn't handle non-finite values.
Results may differ from the reference program's by a relative error of at most 0.0003.
Values may be sent and summed in bfloat16 or wider, within the bound.
A program may use at most 64 MiB of HBM per device.

```python
import math
import jax
import jax.numpy as jnp
from jax import lax

CH_DEV = 128
TRIAL_DEV = 8
PFB_TAPS = 16
LSHIFT = 8
TEMPLATES = 32
TPL_TAPS = 128
STRIDE = 32
WIN = 256
LLEVELS = 7
XLEVELS = 3
CHANNELS = 1024
TRIALS = 64
FRAMES = 8192
N_FREQ = 8


def draw_cross_shift(key, part):
    first_key, second_key = jax.random.split(jax.random.fold_in(key, 17))
    raw_bits = jax.random.randint(first_key, (XLEVELS, TRIALS), 0, 1 << 20)
    limits = TRIAL_DEV * 2 ** jnp.arange(XLEVELS, dtype=jnp.int32)
    values = raw_bits % limits[:, None]
    peak_spot = jax.random.randint(second_key, (XLEVELS, 1), 0, TRIALS)
    column_ids = jnp.arange(TRIALS, dtype=jnp.int32)[None, :]
    return jnp.where(column_ids == peak_spot, limits[:, None] - 1, values).astype(jnp.int32)


def with_ends(values, stream_key, low, largest):
    dims = values.shape
    place = [jax.random.randint(jax.random.fold_in(stream_key, axis), (), 0, dims[axis]) for axis in range(len(dims))]
    values = values.at[tuple(place)].set(low)
    longest = dims.index(max(dims))
    place[longest] = (place[longest] + 1) % dims[longest]
    return values.at[tuple(place)].set(largest)


def levels(rng, extent, shards, low, high):
    level, own = 1.0, jax.random.fold_in(rng, 6)
    for position, blocks in shards:
        draws = jnp.exp(jax.random.uniform(jax.random.fold_in(own, position), (blocks,), jnp.float32, low / len(shards), high / len(shards)))
        level = level * jnp.repeat(draws, extent[position] // blocks).reshape([-1 if axis == position else 1 for axis in range(len(extent))])
    return level


def centred(rng, extent, width, most, pieces=(), held_as=jnp.bfloat16):
    drawn = width * jax.random.normal(rng, extent, jnp.float32)
    if pieces:
        drawn = drawn * levels(rng, extent, pieces, -0.22, 0.18)
    return jnp.clip(drawn, -most, most).astype(held_as)


def setup_inputs(seed: int = 0, part: int = 0) -> dict:
    splits = jax.random.split(jax.random.key(seed), 7)
    part_keys = jax.random.split(jax.random.fold_in(splits[6], part), 7)
    return {
        "voltages": centred(part_keys[0], (2, FRAMES, CHANNELS), 1.0, 6.0, ((1, 2), (2, 8))),
        "pfb_taps": centred(splits[1], (PFB_TAPS, CH_DEV), 0.25, 1.5, (), jnp.float32),
        "local_shift": with_ends(jax.random.randint(splits[2], (LLEVELS, CHANNELS // 2), 0, LSHIFT), jax.random.fold_in(splits[2], 1), 0, LSHIFT - 1).astype(jnp.int32),
        "cross_shift": draw_cross_shift(jax.random.fold_in(splits[6], 71), part),
        "tap_index": with_ends(jax.random.randint(splits[4], (TEMPLATES, TPL_TAPS), 0, WIN), jax.random.fold_in(splits[4], 1), 0, WIN - 1).astype(jnp.int32),
        "tap_weight": centred(splits[5], (TEMPLATES, TPL_TAPS), TPL_TAPS ** -0.5, 0.5, (), jnp.float32),
    }


def filter_taps(padded, pfb_taps, length):

    def add_tap(tap_step, running):
        sliced = lax.dynamic_slice_in_dim(padded, PFB_TAPS - 1 - tap_step, length, axis=1)
        weight = lax.dynamic_index_in_dim(pfb_taps, tap_step, 0, keepdims=False)
        return running + sliced * weight
    shape_zero = jnp.zeros((2, length, padded.shape[2]), jnp.float32)
    return lax.fori_loop(0, PFB_TAPS, add_tap, shape_zero)

def delayed(source, shifts, offset, length):
    frame_ids = jnp.arange(length, dtype=jnp.int32)
    lookup = offset + frame_ids - shifts[..., None].astype(jnp.int32)
    inside = lookup >= 0
    picked = jnp.take_along_axis(source, jnp.maximum(lookup, 0), axis=-1)
    return jnp.where(inside, picked, jnp.zeros_like(picked))

def merge_pairs(series, shifts, trials):
    paired = series.reshape(series.shape[0] // 2, 2, series.shape[1], series.shape[2])
    leading = paired[:, 0]
    trailing = paired[:, 1]
    if trials > series.shape[1]:
        leading = jnp.concatenate([leading, leading], axis=1)
        trailing = jnp.concatenate([trailing, trailing], axis=1)
    return leading + delayed(trailing, shifts, 0, series.shape[2])

def local_fdmt(powers, shift_table):
    series = powers[:, None, :]
    for level_index in range(1, LLEVELS + 1):
        trials = max(1, TRIAL_DEV * 2 ** level_index // CH_DEV)
        band_count = CH_DEV // 2 ** level_index
        shifts = shift_table[level_index - 1].reshape(band_count, 2 ** (level_index - 1))[:, :trials]
        series = merge_pairs(series, shifts, trials)
    return series[0]

def band_power(band_volts, pfb_taps):
    frame_count = band_volts.shape[1]
    padded = jnp.pad(band_volts.astype(jnp.float32), ((0, 0), (PFB_TAPS - 1, 0), (0, 0)))
    filtered = filter_taps(padded, pfb_taps, frame_count)
    spectrum = jnp.fft.fft(filtered[0] + 1j * filtered[1], axis=-1)
    powers = (jnp.real(spectrum) ** 2 + jnp.imag(spectrum) ** 2) / CH_DEV
    powers = powers.T
    return powers - lax.optimization_barrier(jnp.mean(powers, axis=1, keepdims=True))

def template_matrix(tap_index, tap_weight):
    matches = (tap_index[:, :, None] == jnp.arange(WIN, dtype=jnp.int32)[None, None, :]).astype(jnp.float32)
    return jnp.einsum('nik,ni->nk', matches, tap_weight.astype(jnp.float32), precision=lax.Precision.HIGHEST)

def correlate(extended, matrix, positions):
    blocks = extended.reshape(extended.shape[0], -1, STRIDE)
    running = jnp.zeros((extended.shape[0], matrix.shape[0], positions), jnp.float32)
    for block_step in range(WIN // STRIDE):
        running = running + jnp.einsum('rjs,ns->rnj', blocks[:, block_step:block_step + positions], matrix[:, block_step * STRIDE:(block_step + 1) * STRIDE], precision=lax.Precision.HIGHEST)
    return running

def reference(voltages, pfb_taps, local_shift, cross_shift, tap_index, tap_weight):
    frame_count = voltages.shape[1]
    band_volts = voltages.reshape(2, frame_count, N_FREQ, CH_DEV).transpose(2, 0, 1, 3)
    band_tables = local_shift.reshape(LLEVELS, N_FREQ, CH_DEV // 2).transpose(1, 0, 2)

    def one_band(band_item):
        return local_fdmt(band_power(band_item[0], pfb_taps), band_item[1])
    series = lax.map(one_band, (band_volts, band_tables))
    for level_index in range(XLEVELS):
        trials = TRIAL_DEV * 2 ** (level_index + 1)
        shifts = cross_shift[level_index].reshape(N_FREQ // 2 ** (level_index + 1), trials)
        series = merge_pairs(series, shifts, trials)
    dedispersed = series[0] * (1.0 / math.sqrt(CHANNELS))
    extended = jnp.pad(dedispersed, ((0, 0), (0, WIN - STRIDE)))
    matrix = template_matrix(tap_index, tap_weight)
    scores = correlate(extended, matrix, frame_count // STRIDE)
    return (dedispersed, scores)
```

```python
import functools
import math

import jax
import jax.numpy as jnp
import numpy as np
from jax import lax
from jax.experimental import pallas as pl
from jax.experimental.pallas import tpu as pltpu
from jax.sharding import PartitionSpec as P

TRIAL_DEV = 8
PFB_TAPS = 16
LSHIFT = 8
STRIDE = 32
WIN = 256
LLEVELS = 7
LHALO = 56
LANES = 128
PAD = 16
BLOCK = 1024
PIECES = 4
MESH = pl.DeviceIdType.MESH
F32 = jnp.float32
BF16 = jnp.bfloat16


def split(x):
    hi = x.astype(BF16)
    return hi, (x - hi.astype(F32)).astype(BF16)


def dot(a, b):
    return jnp.dot(a, b, preferred_element_type=F32)


def dft_tables(channels):
    index = np.arange(channels)
    angles = (index[:, None] * index[None, :] % channels) * (2.0 * np.pi / channels)
    cosine, sine = np.cos(angles), np.sin(angles)
    table = np.concatenate(
        [np.concatenate([cosine, -sine], 1), np.concatenate([sine, cosine], 1)], 0
    ).astype(np.float32)
    hi = table.astype(jnp.bfloat16)
    lo = (table - hi.astype(np.float32)).astype(jnp.bfloat16)
    return np.stack([hi, lo])


def delay_tables(channels):
    half = channels // 2
    cols, rows, fine = np.arange(half), np.arange(TRIAL_DEV), np.arange(channels)
    masks, spreads = [], []
    for s in range(1, LLEVELS + 1):
        width = 2 ** (s - 1)
        trials = max(1, TRIAL_DEV * 2**s // channels)
        masks.append(cols[None, :] % width == rows[:, None] % trials)
        upper = fine >> (s - 1) & 1
        spreads.append((cols[:, None] // width == fine[None, :] >> s) & (upper[None, :] == 1))
    return np.stack(masks).astype(np.float32), np.stack(spreads).astype(jnp.bfloat16)


def kernel(
    dims,
    volt_ref, taps_ref, lshift_ref, xshift_ref, index_ref, weight_ref, dft_ref, mask_ref, spread_ref,
    ded_ref, sco_ref,
    raw, tail, xs, power, sums, psums, amat, xt, series, arrived, head, nexthead, toep,
    in_sem, tail_sem, sum_sem, x_send, x_recv, head_sem,
):
    frames, halo, levels, channels, tm_size = dims
    total = halo + frames
    tm = lax.axis_index("tm")
    freq = lax.axis_index("freq")
    other = {"tm": lax.rem(tm + 1, tm_size)}
    piece = frames // PIECES

    copies = [
        pltpu.make_async_copy(
            volt_ref.at[:, pl.ds(i * piece, piece), :], raw.at[:, pl.ds(i * piece, piece), :], in_sem.at[i]
        )
        for i in range(PIECES)
    ]
    for copy in copies:
        copy.start()
    barrier = pltpu.get_barrier_semaphore()
    pl.semaphore_signal(barrier, inc=1, device_id=other, device_id_type=MESH)
    for j in range(levels):
        pl.semaphore_signal(barrier, inc=1, device_id={"freq": freq ^ (1 << j)}, device_id_type=MESH)

    delays = jnp.zeros((TRIAL_DEV, channels), F32)
    for s in range(LLEVELS):
        row = lshift_ref[s : s + 1, :].astype(F32)
        delays = delays + dot((row * mask_ref[s]).astype(BF16), spread_ref[s])
    for b in range(LSHIFT):
        for a in range(LLEVELS):
            at = (b * LLEVELS + a) * TRIAL_DEV
            amat[at : at + TRIAL_DEV, :] = jnp.where(delays == float(a * LSHIFT + b), 1.0, 0.0)

    pl.semaphore_wait(barrier, 1 + levels)
    send_tail = pltpu.make_async_remote_copy(
        src_ref=volt_ref.at[:, pl.ds(frames - halo, halo), :], dst_ref=tail,
        send_sem=tail_sem.at[0], recv_sem=tail_sem.at[1], device_id=other, device_id_type=MESH,
    )
    send_tail.start()

    taps = [taps_ref[k : k + 1, :] for k in range(PFB_TAPS)]

    def channelize(c):
        base = pl.multiple_of(c * LANES, LANES)
        parts = []
        for r in range(2):
            acc = xs[r, pl.ds(base + PAD, LANES), :] * taps[0]
            for k in range(1, PFB_TAPS):
                acc = acc + xs[r, pl.ds(base + PAD - k, LANES), :] * taps[k]
            parts.append(acc)
        hi, lo = split(jnp.concatenate(parts, axis=1))
        spectrum = dot(hi, dft_ref[0]) + dot(hi, dft_ref[1]) + dot(lo, dft_ref[0])
        squared = spectrum * spectrum
        value = (squared[:, :channels] + squared[:, channels:]) * (1.0 / channels)
        power[pl.ds(base, LANES), :] = value
        return value

    def add_sums(c):
        value = channelize(c)
        sums[...] += value.reshape(LANES // 8, 8, channels).sum(0)

    first = halo // LANES
    last = total // LANES

    def convert(c):
        at = pl.multiple_of(c * LANES, LANES)
        for r in range(2):
            xs[r, pl.ds(at + PAD + halo, LANES), :] = raw[r, pl.ds(at, LANES), :].astype(F32)

    sums[...] = jnp.zeros_like(sums)
    per = piece // LANES
    for i in range(PIECES):
        copies[i].wait()
        if i == 0:
            convert(0)

        def main(c, carry):
            convert(c)
            add_sums(c + first)
            return carry

        lax.fori_loop(max(1, i * per), (i + 1) * per, main, 0)

    send_tail.wait()
    inside = (tm > 0).astype(F32)
    for r in range(2):
        xs[r, 0:PAD, :] = jnp.zeros((PAD, channels), F32)
        xs[r, PAD : PAD + halo, :] = tail[r].astype(F32) * inside
    add_sums(first)
    psums[0] = sums[...]
    send_sums = pltpu.make_async_remote_copy(
        src_ref=psums.at[0], dst_ref=psums.at[1],
        send_sem=sum_sem.at[0], recv_sem=sum_sem.at[1], device_id=other, device_id_type=MESH,
    )
    send_sums.start()

    def early(c, carry):
        channelize(c)
        return carry

    lax.fori_loop(0, first, early, 0)
    send_sums.wait()
    mean = jnp.sum(psums[0] + psums[1], axis=0, keepdims=True) * (1.0 / (frames * tm_size))

    def level0(c, carry):
        base = pl.multiple_of(c * LANES, LANES)
        keep = jnp.logical_or(c >= first, tm > 0).astype(F32)
        hi, lo = split(((power[pl.ds(base, LANES), :] - mean) * keep).T)
        xt[0:channels, pl.ds(base, LANES)] = hi
        xt[channels : 2 * channels, pl.ds(base, LANES)] = lo
        return carry

    lax.fori_loop(0, last, level0, 0, unroll=3 if last % 3 == 0 else 1)

    single = amat[...].astype(BF16)
    sorter = jnp.concatenate([single, single], axis=1)
    starts = [0] + [halo + BLOCK * i for i in range(1, frames // BLOCK)]
    ends = starts[1:] + [total]
    rows = LLEVELS * TRIAL_DEV
    for begin, end in zip(starts, ends):
        back = LANES if begin else 0
        sorted_rows = dot(sorter, xt[:, begin - back : end])
        acc = sorted_rows[(LSHIFT - 1) * rows :]
        for b in reversed(range(LSHIFT - 1)):
            acc = pltpu.roll(acc, 1, 1) + sorted_rows[b * rows : (b + 1) * rows]
        out = acc[(LLEVELS - 1) * TRIAL_DEV :]
        for a in reversed(range(LLEVELS - 1)):
            out = pltpu.roll(out, LSHIFT, 1) + acc[a * TRIAL_DEV : (a + 1) * TRIAL_DEV]
        series[0, :, begin:end] = out[:, back:]

    def exchange(j):
        return pltpu.make_async_remote_copy(
            src_ref=series.at[j], dst_ref=arrived.at[j],
            send_sem=x_send.at[j], recv_sem=x_recv.at[j],
            device_id={"freq": freq ^ (1 << j)}, device_id_type=MESH,
        )

    pending = exchange(0)
    pending.start()

    group = LANES // STRIDE
    templates = index_ref.shape[0]
    lane = lax.broadcasted_iota(jnp.int32, (WIN, LANES), 1)
    offset = lax.broadcasted_iota(jnp.int32, (WIN, index_ref.shape[1]), 0)

    def place(n, carry):
        hit = jnp.where(offset == index_ref[pl.ds(n, 1), :], weight_ref[pl.ds(n, 1), :], 0.0)
        column = jnp.sum(hit, axis=1, keepdims=True)
        toep[0:WIN, :] = jnp.where(lax.rem(lane, templates) == n, column, toep[0:WIN, :])
        return carry

    span = toep.shape[0]
    toep[...] = jnp.zeros_like(toep)
    lax.fori_loop(0, templates, place, 0)
    base_rows = toep[0:WIN, :]
    placed = jnp.zeros((span, LANES), F32)
    for i in range(group):
        mine = jnp.where(lane // templates == i, base_rows, 0.0)
        placed = placed + jnp.concatenate(
            ([jnp.zeros((STRIDE * i, LANES), F32)] if i else [])
            + [mine, jnp.zeros((span - WIN - STRIDE * i, LANES), F32)], axis=0
        )
    toep_hi, toep_lo = split(placed)

    eye = lax.broadcasted_iota(jnp.int32, (TRIAL_DEV, TRIAL_DEV), 0) == lax.broadcasted_iota(
        jnp.int32, (TRIAL_DEV, TRIAL_DEV), 1
    )
    current = None
    for j in range(levels):
        shift_row = jnp.broadcast_to(xshift_ref[j : j + 1, :].astype(F32), (TRIAL_DEV, TRIAL_DEV))
        shifts = jnp.sum(jnp.where(eye, shift_row, 0.0), axis=1, keepdims=True).astype(jnp.int32)
        pending.wait()
        upper = ((freq >> j) & 1).astype(F32) > 0.5
        mine, theirs = series[j], arrived[j]
        leading = jnp.where(upper, theirs, mine)
        trailing = jnp.where(upper, mine, theirs)
        for bit in range((TRIAL_DEV << j).bit_length() - 1):
            trailing = jnp.where(
                ((shifts >> bit) & 1) == 1, pltpu.roll(trailing, 1 << bit, 1), trailing
            )
        current = leading + trailing
        if j + 1 < levels:
            series[j + 1] = current
            pending = exchange(j + 1)
            pending.start()

    factor = 1.0 / math.sqrt(channels << levels)
    dedispersed = current[:, halo:] * factor
    head[...] = dedispersed[:, :WIN]
    send_head = pltpu.make_async_remote_copy(
        src_ref=head, dst_ref=nexthead,
        send_sem=head_sem.at[0], recv_sem=head_sem.at[1], device_id=other, device_id_type=MESH,
    )
    send_head.start()
    ded_ref[...] = dedispersed
    send_head.wait()
    follow = nexthead[...] * (tm < tm_size - 1).astype(F32)
    wide = jnp.concatenate([dedispersed, follow], axis=1)
    count = frames // LANES
    tiles = [wide[:, q * LANES : (q + 1) * LANES] for q in range(count + span // LANES - 1)]
    stacked = jnp.concatenate(
        [jnp.concatenate(tiles[u : u + count], axis=0) for u in range(span // LANES)], axis=1
    )
    hi, lo = split(stacked)
    sco_ref[...] = dot(hi, toep_hi) + dot(hi, toep_lo) + dot(lo, toep_hi)


def solution(mesh):
    freq_size, tm_size = mesh.shape["freq"], mesh.shape["tm"]
    levels = freq_size.bit_length() - 1
    reach = PFB_TAPS - 1 + LHALO + TRIAL_DEV * (freq_size - 1)
    halo = -(-reach // LANES) * LANES

    def on_device(voltages, pfb_taps, local_shift, cross_shift, tap_index, tap_weight):
        frames, channels = voltages.shape[1:]
        templates = tap_index.shape[0]
        total = halo + frames
        span = WIN + LANES
        mask, spread = delay_tables(channels)
        vmem = pl.BlockSpec(memory_space=pltpu.VMEM)
        groups = frames // LANES
        dedispersed, scores = pl.pallas_call(
            functools.partial(kernel, (frames, halo, levels, channels, tm_size)),
            out_shape=(
                jax.ShapeDtypeStruct((TRIAL_DEV, frames), F32),
                jax.ShapeDtypeStruct((groups * TRIAL_DEV, LANES), F32),
            ),
            in_specs=[pl.BlockSpec(memory_space=pl.ANY)] + [vmem] * 8,
            out_specs=(vmem, vmem),
            scratch_shapes=[
                pltpu.VMEM((2, frames, channels), BF16),
                pltpu.VMEM((2, halo, channels), BF16),
                pltpu.VMEM((2, PAD + total, channels), F32),
                pltpu.VMEM((total, channels), F32),
                pltpu.VMEM((8, channels), F32),
                pltpu.VMEM((2, 8, channels), F32),
                pltpu.VMEM((LSHIFT * LLEVELS * TRIAL_DEV, channels), F32),
                pltpu.VMEM((2 * channels, total), BF16),
                pltpu.VMEM((levels, TRIAL_DEV, total), F32),
                pltpu.VMEM((levels, TRIAL_DEV, total), F32),
                pltpu.VMEM((TRIAL_DEV, WIN), F32),
                pltpu.VMEM((TRIAL_DEV, WIN), F32),
                pltpu.VMEM((span, LANES), F32),
                pltpu.SemaphoreType.DMA((PIECES,)),
                pltpu.SemaphoreType.DMA((2,)),
                pltpu.SemaphoreType.DMA((2,)),
                pltpu.SemaphoreType.DMA((levels,)),
                pltpu.SemaphoreType.DMA((levels,)),
                pltpu.SemaphoreType.DMA((2,)),
            ],
            compiler_params=pltpu.CompilerParams(collective_id=0, has_side_effects=True),
        )(
            voltages, pfb_taps, local_shift, cross_shift, tap_index, tap_weight,
            jnp.asarray(dft_tables(channels)), jnp.asarray(mask), jnp.asarray(spread),
        )
        placed = scores.reshape(groups, TRIAL_DEV, LANES // STRIDE, templates)
        placed = placed.transpose(1, 3, 0, 2).reshape(TRIAL_DEV, templates, frames // STRIDE)
        return dedispersed, placed

    return jax.shard_map(
        on_device,
        mesh=mesh,
        in_specs=(P("beam", "tm", "freq"), P(), P(None, "freq"), P(None, "freq"), P(), P()),
        out_specs=(P(("beam", "freq"), "tm"), P(("beam", "freq"), None, "tm")),
        check_vma=False,
    )
```

```python
import functools
import math

import jax
import jax.numpy as jnp
import numpy as np
from jax import lax
from jax.experimental import pallas as pl
from jax.experimental.pallas import tpu as pltpu
from jax.sharding import PartitionSpec as P

TRIAL_DEV = 8
PFB_TAPS = 16
LSHIFT = 8
STRIDE = 32
WIN = 256
LLEVELS = 7
LHALO = 56
LANES = 128
PAD = 16
SMALL = 4
BLOCKS = 3
MESH = pl.DeviceIdType.MESH
F32 = jnp.float32
BF16 = jnp.bfloat16


def split(x):
    hi = x.astype(BF16)
    return hi, (x - hi.astype(F32)).astype(BF16)


def dot(a, b):
    return jnp.dot(a, b, preferred_element_type=F32)


def dft_tables(channels):
    index = np.arange(channels)
    angles = (index[:, None] * index[None, :] % channels) * (2.0 * np.pi / channels)
    cosine, sine = np.cos(angles), np.sin(angles)
    table = np.concatenate(
        [np.concatenate([cosine, -sine], 1), np.concatenate([sine, cosine], 1)], 0
    ).astype(np.float32)
    hi = table.astype(jnp.bfloat16)
    lo = (table - hi.astype(np.float32)).astype(jnp.bfloat16)
    return np.stack([hi, lo])


def delay_tables(channels):
    half = channels // 2
    cols, rows, fine = np.arange(half), np.arange(TRIAL_DEV), np.arange(channels)
    masks, spreads = [], []
    for s in range(1, LLEVELS + 1):
        width = 2 ** (s - 1)
        trials = max(1, TRIAL_DEV * 2**s // channels)
        masks.append(cols[None, :] % width == rows[:, None] % trials)
        upper = fine >> (s - 1) & 1
        spreads.append((cols[:, None] // width == fine[None, :] >> s) & (upper[None, :] == 1))
    return np.stack(masks).astype(np.float32), np.stack(spreads).astype(jnp.bfloat16)


def plan(frames, halo, context, reach):
    chunks, first = frames // LANES, halo // LANES
    small = max(SMALL, -(-reach // LANES))
    cuts = [small + (chunks - small) * i // BLOCKS for i in range(BLOCKS + 1)]
    spans = [(0, small)] + list(zip(cuts[:-1], cuts[1:]))
    return [(first + lo, first + hi) for lo, hi in spans]


def kernel(
    dims, blocks, offsets,
    volt_ref, taps_ref, lshift_ref, xshift_ref, index_ref, weight_ref, dft_hbm, mask_hbm, spread_hbm,
    ded_ref, sco_ref,
    raw, tail, xs, power, sums, psums, amat, xt, series, arrived, final, head, nexthead, toep,
    dft_ref, mask_ref, spread_ref,
    in_sem, table_sem, tail_sem, sum_sem, x_send, x_recv, head_sem,
):
    frames, halo, context, levels, channels, tm_size = dims
    first = halo // LANES
    back = context // LANES
    before = back + 1
    tm = lax.axis_index("tm")
    freq = lax.axis_index("freq")
    other = {"tm": lax.rem(tm + 1, tm_size)}
    order = list(range(1, len(blocks))) + [0]
    begin_pre = blocks[1][0] - before
    lead = max(begin_pre - 1 - first, 0) * LANES

    pieces = []
    for at, k in enumerate(order):
        lo = lead if at == 0 else (blocks[k][0] - first) * LANES
        hi = (blocks[k][1] - first) * LANES if k else lead
        pieces.append((0 if k == 0 else lo, hi))
    copies = [
        pltpu.make_async_copy(volt_ref.at[:, pl.ds(lo, hi - lo), :], raw.at[:, pl.ds(lo, hi - lo), :], in_sem.at[i])
        if hi > lo else None
        for i, (lo, hi) in enumerate(pieces)
    ]
    tables = [
        pltpu.make_async_copy(src, dst, table_sem.at[i])
        for i, (src, dst) in enumerate([(dft_hbm, dft_ref), (mask_hbm, mask_ref), (spread_hbm, spread_ref)])
    ]
    copies[0].start()
    for table in tables:
        table.start()
    for copy in copies[1:]:
        if copy is not None:
            copy.start()
    barrier = pltpu.get_barrier_semaphore()
    pl.semaphore_signal(barrier, inc=1, device_id=other, device_id_type=MESH)
    for j in range(levels):
        pl.semaphore_signal(barrier, inc=1, device_id={"freq": freq ^ (1 << j)}, device_id_type=MESH)
    pl.semaphore_wait(barrier, 1 + levels)
    send_tail = pltpu.make_async_remote_copy(
        src_ref=volt_ref.at[:, pl.ds(frames - halo, halo), :], dst_ref=tail,
        send_sem=tail_sem.at[0], recv_sem=tail_sem.at[1], device_id=other, device_id_type=MESH,
    )
    send_tail.start()

    for table in tables:
        table.wait()
    delays = jnp.zeros((TRIAL_DEV, channels), F32)
    for s in range(LLEVELS):
        row = lshift_ref[s : s + 1, :].astype(F32)
        delays = delays + dot((row * mask_ref[s]).astype(BF16), spread_ref[s])
    for b in range(LSHIFT):
        for a in range(LLEVELS):
            at = (b * LLEVELS + a) * TRIAL_DEV
            amat[at : at + TRIAL_DEV, :] = jnp.where(delays == float(a * LSHIFT + b), 1.0, 0.0)

    taps = [taps_ref[k : k + 1, :] for k in range(PFB_TAPS)]

    def channelize(c):
        base = pl.multiple_of(c * LANES, LANES)
        parts = []
        for r in range(2):
            acc = xs[r, pl.ds(base + PAD, LANES), :] * taps[0]
            for k in range(1, PFB_TAPS):
                acc = acc + xs[r, pl.ds(base + PAD - k, LANES), :] * taps[k]
            parts.append(acc)
        hi, lo = split(jnp.concatenate(parts, axis=1))
        spectrum = dot(hi, dft_ref[0]) + dot(hi, dft_ref[1]) + dot(lo, dft_ref[0])
        squared = spectrum * spectrum
        return (squared[:, :channels] + squared[:, channels:]) * (1.0 / channels)

    def store_columns(c, value):
        base = pl.multiple_of(c * LANES, LANES)
        hi, lo = split(value.T)
        xt[0:channels, pl.ds(base, LANES)] = hi
        xt[channels : 2 * channels, pl.ds(base, LANES)] = lo

    def add_sums(value):
        sums[...] += value.reshape(LANES // 8, 8, channels).sum(0)

    def convert(c):
        at = pl.multiple_of(c * LANES, LANES)
        source = pl.multiple_of(at - halo, LANES)
        for r in range(2):
            xs[r, pl.ds(at + PAD, LANES), :] = raw[r, pl.ds(source, LANES), :].astype(F32)

    def plain(c, carry):
        convert(c)
        value = channelize(c)
        add_sums(value)
        store_columns(c, value)
        return carry

    def keep_power(c, value):
        power[pl.ds(pl.multiple_of(c * LANES, LANES), LANES), :] = value

    def shared(c, carry):
        convert(c)
        value = channelize(c)
        add_sums(value)
        store_columns(c, value)
        keep_power(c, value)
        return carry

    def opening(c, carry):
        convert(c)
        value = channelize(c)
        add_sums(value)
        keep_power(c, value)
        return carry

    def early(c, carry):
        keep_power(c, channelize(c))
        return carry

    sums[...] = jnp.zeros_like(sums)
    rows = LLEVELS * TRIAL_DEV

    def width(k):
        return (blocks[k][1] - blocks[k][0]) * LANES + context

    def merge_local(k):
        end = blocks[k][1] * LANES
        begin = end - width(k)
        extra = min(LANES, begin)
        single = amat[...].astype(BF16)
        sorter = jnp.concatenate([single, single], axis=1)
        sorted_rows = dot(sorter, xt[:, begin - extra : end])
        acc = sorted_rows[(LSHIFT - 1) * rows :]
        for b in reversed(range(LSHIFT - 1)):
            acc = pltpu.roll(acc, 1, 1) + sorted_rows[b * rows : (b + 1) * rows]
        out = acc[(LLEVELS - 1) * TRIAL_DEV :]
        for a in reversed(range(LLEVELS - 1)):
            out = pltpu.roll(out, LSHIFT, 1) + acc[a * TRIAL_DEV : (a + 1) * TRIAL_DEV]
        series[0, :, offsets[k] : offsets[k] + width(k)] = out[:, extra:]

    def exchange(j, k):
        size = width(k) + (LANES if k == 0 else 0)
        where = pl.ds(offsets[k], size)
        return pltpu.make_async_remote_copy(
            src_ref=series.at[j, :, where], dst_ref=arrived.at[j, :, where],
            send_sem=x_send.at[j, k], recv_sem=x_recv.at[j, k],
            device_id={"freq": freq ^ (1 << j)}, device_id_type=MESH,
        )

    eye = lax.broadcasted_iota(jnp.int32, (TRIAL_DEV, TRIAL_DEV), 0) == lax.broadcasted_iota(
        jnp.int32, (TRIAL_DEV, TRIAL_DEV), 1
    )
    shift_cols = []
    for j in range(levels):
        shift_row = jnp.broadcast_to(xshift_ref[j : j + 1, :].astype(F32), (TRIAL_DEV, TRIAL_DEV))
        shift_cols.append(jnp.sum(jnp.where(eye, shift_row, 0.0), axis=1, keepdims=True).astype(jnp.int32))

    def merge_across(j, k):
        exchange(j, k).wait()
        here = slice(offsets[k], offsets[k] + width(k))
        upper = ((freq >> j) & 1) == 1
        mine, theirs = series[j, :, here], arrived[j, :, here]
        leading = jnp.where(upper, theirs, mine)
        trailing = jnp.where(upper, mine, theirs)
        for bit in range((TRIAL_DEV << j).bit_length() - 1):
            trailing = jnp.where(
                ((shift_cols[j] >> bit) & 1) == 1, pltpu.roll(trailing, 1 << bit, 1), trailing
            )
        merged = leading + trailing
        if k == 0:
            past = slice(here.stop, here.stop + LANES)
            totals = series[j, :, past] + arrived[j, :, past]
        if j + 1 < levels:
            series[j + 1, :, here] = merged
            if k == 0:
                series[j + 1, :, past] = totals
            exchange(j + 1, k).start()
        else:
            lo, hi = ((c - first) * LANES for c in blocks[k])
            final[:, lo:hi] = merged[:, context:]
            if k == 0:
                final[:, frames : frames + LANES] = totals

    ready = []

    def advance():
        moved = ready[:]
        ready.clear()
        for j, k in moved:
            merge_across(j, k)
            if j + 1 < levels:
                ready.append((j + 1, k))

    def take_tail():
        send_tail.wait()
        inside = (tm > 0).astype(F32)
        for r in range(2):
            xs[r, 0:PAD, :] = jnp.zeros((PAD, channels), F32)
            xs[r, PAD : PAD + halo, :] = tail[r].astype(F32) * inside

    late_tail = begin_pre > first
    copies[0].wait()
    if late_tail:
        convert(begin_pre - 1)
    else:
        take_tail()
    lax.fori_loop(begin_pre, blocks[1][0], shared, 0)
    for at, k in enumerate(order[:-1]):
        if at:
            copies[at].wait()
        lax.fori_loop(blocks[k][0], blocks[k][1], plain, 0)
        merge_local(k)
        exchange(0, k).start()
        advance()
        ready.append((0, k))

    if late_tail:
        if copies[-1] is not None:
            copies[-1].wait()
        take_tail()
        lax.fori_loop(first, begin_pre, opening, 0)
    psums[0] = sums[...]
    send_sums = pltpu.make_async_remote_copy(
        src_ref=psums.at[0], dst_ref=psums.at[1],
        send_sem=sum_sem.at[0], recv_sem=sum_sem.at[1], device_id=other, device_id_type=MESH,
    )
    send_sums.start()
    lax.fori_loop(0, first, early, 0)
    send_sums.wait()
    mean = jnp.sum(psums[0] + psums[1], axis=0, keepdims=True) * (1.0 / (frames * tm_size))

    def level0(c, carry):
        base = pl.multiple_of(c * LANES, LANES)
        keep = jnp.logical_or(c >= first, tm > 0).astype(F32)
        store_columns(c, (power[pl.ds(base, LANES), :] - mean) * keep)
        return carry

    lax.fori_loop(0, blocks[0][1], level0, 0, unroll=5 if blocks[0][1] % 5 == 0 else 1)
    merge_local(0)
    band_total = jnp.broadcast_to(jnp.sum(mean, axis=1, keepdims=True), (TRIAL_DEV, LANES))
    series[0, :, offsets[0] + width(0) : offsets[0] + width(0) + LANES] = band_total
    exchange(0, 0).start()
    advance()
    ready.append((0, 0))

    group = LANES // STRIDE
    templates = index_ref.shape[0]
    lane = lax.broadcasted_iota(jnp.int32, (WIN, LANES), 1)
    offset = lax.broadcasted_iota(jnp.int32, (WIN, index_ref.shape[1]), 0)

    def place(n, carry):
        hit = jnp.where(offset == index_ref[pl.ds(n, 1), :], weight_ref[pl.ds(n, 1), :], 0.0)
        column = jnp.sum(hit, axis=1, keepdims=True)
        toep[0:WIN, :] = jnp.where(lax.rem(lane, templates) == n, column, toep[0:WIN, :])
        return carry

    span = toep.shape[0]
    toep[...] = jnp.zeros_like(toep)
    steps = levels + 1
    done = 0
    while ready:
        upto = min(templates, done + -(-templates // steps))
        lax.fori_loop(done, upto, place, 0)
        done = upto
        advance()
    lax.fori_loop(done, templates, place, 0)
    base_rows = toep[0:WIN, :]
    placed = jnp.zeros((span, LANES), F32)
    for i in range(group):
        mine = jnp.where(lane // templates == i, base_rows, 0.0)
        placed = placed + jnp.concatenate(
            ([jnp.zeros((STRIDE * i, LANES), F32)] if i else [])
            + [mine, jnp.zeros((span - WIN - STRIDE * i, LANES), F32)], axis=0
        )
    toep_hi, toep_lo = split(placed)

    factor = 1.0 / math.sqrt(channels << levels)
    head[...] = final[:, 0:WIN] * factor
    send_head = pltpu.make_async_remote_copy(
        src_ref=head, dst_ref=nexthead,
        send_sem=head_sem.at[0], recv_sem=head_sem.at[1], device_id=other, device_id_type=MESH,
    )
    send_head.start()
    opened = (blocks[0][1] - first) * LANES
    total_mean = jnp.broadcast_to(final[:, frames : frames + 1], (TRIAL_DEV, frames - opened))
    dedispersed = jnp.concatenate([final[:, 0:opened], final[:, opened:frames] - total_mean], axis=1) * factor
    ded_ref[...] = dedispersed
    count = frames // LANES

    def correlate(wide, number):
        tiles = [wide[:, q * LANES : (q + 1) * LANES] for q in range(number + span // LANES - 1)]
        stacked = jnp.concatenate(
            [jnp.concatenate(tiles[u : u + number], axis=0) for u in range(span // LANES)], axis=1
        )
        hi, lo = split(stacked)
        return dot(hi, toep_hi) + dot(hi, toep_lo) + dot(lo, toep_hi)

    part = count - 4
    sco_ref[0 : part * TRIAL_DEV, :] = correlate(dedispersed, part)
    send_head.wait()
    follow = nexthead[...] * (tm < tm_size - 1).astype(F32)
    sco_ref[part * TRIAL_DEV :, :] = correlate(
        jnp.concatenate([dedispersed[:, part * LANES :], follow], axis=1), count - part
    )


def solution(mesh):
    freq_size, tm_size = mesh.shape["freq"], mesh.shape["tm"]
    levels = freq_size.bit_length() - 1
    reach = PFB_TAPS - 1 + LHALO + TRIAL_DEV * (freq_size - 1)
    halo = -(-reach // LANES) * LANES
    context = -(-TRIAL_DEV * (freq_size - 1) // LANES) * LANES

    def on_device(voltages, pfb_taps, local_shift, cross_shift, tap_index, tap_weight):
        frames, channels = voltages.shape[1:]
        templates = tap_index.shape[0]
        total = halo + frames
        span = WIN + LANES
        blocks = plan(frames, halo, context, reach)
        offsets, room = [], 0
        for k, (lo, hi) in enumerate(blocks):
            offsets.append(room)
            room += (hi - lo) * LANES + context + (LANES if k == 0 else 0)
        mask, spread = delay_tables(channels)
        vmem = pl.BlockSpec(memory_space=pltpu.VMEM)
        hbm = pl.BlockSpec(memory_space=pl.ANY)
        groups = frames // LANES
        dft = dft_tables(channels)
        dedispersed, scores = pl.pallas_call(
            functools.partial(kernel, (frames, halo, context, levels, channels, tm_size), blocks, offsets),
            out_shape=(
                jax.ShapeDtypeStruct((TRIAL_DEV, frames), F32),
                jax.ShapeDtypeStruct((groups * TRIAL_DEV, LANES), F32),
            ),
            in_specs=[hbm] + [vmem] * 5 + [hbm] * 3,
            out_specs=(vmem, vmem),
            scratch_shapes=[
                pltpu.VMEM((2, frames, channels), BF16),
                pltpu.VMEM((2, halo, channels), BF16),
                pltpu.VMEM((2, PAD + total, channels), F32),
                pltpu.VMEM((blocks[0][1] * LANES, channels), F32),
                pltpu.VMEM((8, channels), F32),
                pltpu.VMEM((2, 8, channels), F32),
                pltpu.VMEM((LSHIFT * LLEVELS * TRIAL_DEV, channels), F32),
                pltpu.VMEM((2 * channels, total), BF16),
                pltpu.VMEM((levels, TRIAL_DEV, room), F32),
                pltpu.VMEM((levels, TRIAL_DEV, room), F32),
                pltpu.VMEM((TRIAL_DEV, frames + LANES), F32),
                pltpu.VMEM((TRIAL_DEV, WIN), F32),
                pltpu.VMEM((TRIAL_DEV, WIN), F32),
                pltpu.VMEM((span, LANES), F32),
                pltpu.VMEM(dft.shape, BF16),
                pltpu.VMEM(mask.shape, F32),
                pltpu.VMEM(spread.shape, BF16),
                pltpu.SemaphoreType.DMA((len(blocks),)),
                pltpu.SemaphoreType.DMA((3,)),
                pltpu.SemaphoreType.DMA((2,)),
                pltpu.SemaphoreType.DMA((2,)),
                pltpu.SemaphoreType.DMA((levels, len(blocks))),
                pltpu.SemaphoreType.DMA((levels, len(blocks))),
                pltpu.SemaphoreType.DMA((2,)),
            ],
            compiler_params=pltpu.CompilerParams(collective_id=0, has_side_effects=True),
        )(
            voltages, pfb_taps, local_shift, cross_shift, tap_index, tap_weight,
            jnp.asarray(dft), jnp.asarray(mask), jnp.asarray(spread),
        )
        placed = scores.reshape(groups, TRIAL_DEV, LANES // STRIDE, templates)
        placed = placed.transpose(1, 3, 0, 2).reshape(TRIAL_DEV, templates, frames // STRIDE)
        return dedispersed, placed

    return jax.shard_map(
        on_device,
        mesh=mesh,
        in_specs=(P("beam", "tm", "freq"), P(), P(None, "freq"), P(None, "freq"), P(), P()),
        out_specs=(P(("beam", "freq"), "tm"), P(("beam", "freq"), None, "tm")),
        check_vma=False,
    )
```

```python
import functools
import math

import jax
import jax.numpy as jnp
import numpy as np
from jax import lax
from jax.experimental import pallas as pl
from jax.experimental.pallas import tpu as pltpu
from jax.sharding import PartitionSpec as P

TRIAL_DEV = 8
PFB_TAPS = 16
LSHIFT = 8
STRIDE = 32
WIN = 256
LLEVELS = 7
LHALO = 56
LANES = 128
PAD = 16
SMALL = 4
BLOCKS = 2
UNROLL = 14
MESH = pl.DeviceIdType.MESH
F32 = jnp.float32
BF16 = jnp.bfloat16


REACH = LLEVELS * (LSHIFT - 1)
ROW = [0]
for _step in range(LSHIFT):
    ROW.append(ROW[-1] + TRIAL_DEV * ((REACH - _step) // LSHIFT + 1))


def split(x):
    hi = x.astype(BF16)
    return hi, (x - hi.astype(F32)).astype(BF16)


def dot(a, b):
    return jnp.dot(a, b, preferred_element_type=F32)


def dft_tables(channels):
    index = np.arange(channels)
    angles = (index[:, None] * index[None, :] % channels) * (2.0 * np.pi / channels)
    cosine, sine = np.cos(angles), np.sin(angles)
    table = np.concatenate(
        [np.concatenate([cosine, -sine], 1), np.concatenate([sine, cosine], 1)], 0
    ).astype(np.float32)
    hi = table.astype(jnp.bfloat16)
    lo = (table - hi.astype(np.float32)).astype(jnp.bfloat16)
    return np.stack([hi, lo])


def delay_tables(channels):
    half = channels // 2
    cols, rows, fine = np.arange(half), np.arange(TRIAL_DEV), np.arange(channels)
    masks, spreads = [], []
    for s in range(1, LLEVELS + 1):
        width = 2 ** (s - 1)
        trials = max(1, TRIAL_DEV * 2**s // channels)
        masks.append(cols[None, :] % width == rows[:, None] % trials)
        upper = fine >> (s - 1) & 1
        spreads.append((cols[:, None] // width == fine[None, :] >> s) & (upper[None, :] == 1))
    return np.stack(masks).astype(np.float32), np.stack(spreads).astype(jnp.bfloat16)


def plan(frames, halo, context, reach):
    chunks, first = frames // LANES, halo // LANES
    small = max(SMALL, -(-reach // LANES))
    cuts = [small + (chunks - small) * i // BLOCKS for i in range(BLOCKS + 1)]
    spans = [(0, small)] + list(zip(cuts[:-1], cuts[1:]))
    return [(first + lo, first + hi) for lo, hi in spans]


def kernel(
    dims, blocks, offsets,
    volt_ref, taps_ref, lshift_ref, xshift_ref, index_ref, weight_ref, dft_hbm, mask_hbm, spread_hbm,
    ded_ref, sco_ref,
    raw, tail, xs, power, sums, psums, amat, xt, series, arrived, final, head, nexthead, toep,
    dft_ref, mask_ref, spread_ref,
    in_sem, table_sem, tail_sem, sum_sem, x_send, x_recv, head_sem,
):
    frames, halo, context, levels, channels, tm_size = dims
    first = halo // LANES
    back = context // LANES
    before = back + 1
    tm = lax.axis_index("tm")
    freq = lax.axis_index("freq")
    other = {"tm": lax.rem(tm + 1, tm_size)}
    order = list(range(1, len(blocks))) + [0]
    begin_pre = blocks[1][0] - before
    lead = max(begin_pre - 1 - first, 0) * LANES

    pieces = []
    for at, k in enumerate(order):
        lo = lead if at == 0 else (blocks[k][0] - first) * LANES
        hi = (blocks[k][1] - first) * LANES if k else lead
        pieces.append((0 if k == 0 else lo, hi))
    copies = [
        pltpu.make_async_copy(volt_ref.at[:, pl.ds(lo, hi - lo), :], raw.at[:, pl.ds(lo, hi - lo), :], in_sem.at[i])
        if hi > lo else None
        for i, (lo, hi) in enumerate(pieces)
    ]
    tables = [
        pltpu.make_async_copy(src, dst, table_sem.at[i])
        for i, (src, dst) in enumerate([(dft_hbm, dft_ref), (mask_hbm, mask_ref), (spread_hbm, spread_ref)])
    ]
    copies[0].start()
    for table in tables:
        table.start()
    for copy in copies[1:]:
        if copy is not None:
            copy.start()
    barrier = pltpu.get_barrier_semaphore()
    pl.semaphore_signal(barrier, inc=1, device_id=other, device_id_type=MESH)
    for j in range(levels):
        pl.semaphore_signal(barrier, inc=1, device_id={"freq": freq ^ (1 << j)}, device_id_type=MESH)
    pl.semaphore_wait(barrier, 1 + levels)
    send_tail = pltpu.make_async_remote_copy(
        src_ref=volt_ref.at[:, pl.ds(frames - halo, halo), :], dst_ref=tail,
        send_sem=tail_sem.at[0], recv_sem=tail_sem.at[1], device_id=other, device_id_type=MESH,
    )
    send_tail.start()

    for table in tables:
        table.wait()
    delays = jnp.zeros((TRIAL_DEV, channels), F32)
    for s in range(LLEVELS):
        row = lshift_ref[s : s + 1, :].astype(F32)
        delays = delays + dot((row * mask_ref[s]).astype(BF16), spread_ref[s])
    for b in range(LSHIFT):
        for a in range(LLEVELS):
            if a * LSHIFT + b > REACH:
                continue
            at = ROW[b] + a * TRIAL_DEV
            amat[at : at + TRIAL_DEV, :] = jnp.where(delays == float(a * LSHIFT + b), 1.0, 0.0)

    taps = [taps_ref[k : k + 1, :] for k in range(PFB_TAPS)]

    def channelize(c):
        base = pl.multiple_of(c * LANES, LANES)
        parts = []
        for r in range(2):
            acc = xs[r, pl.ds(base + PAD, LANES), :] * taps[0]
            for k in range(1, PFB_TAPS):
                acc = acc + xs[r, pl.ds(base + PAD - k, LANES), :] * taps[k]
            parts.append(acc)
        hi, lo = split(jnp.concatenate(parts, axis=1))
        spectrum = dot(hi, dft_ref[0]) + dot(hi, dft_ref[1]) + dot(lo, dft_ref[0])
        squared = spectrum * spectrum
        return (squared[:, :channels] + squared[:, channels:]) * (1.0 / channels)

    def store_columns(c, value):
        base = pl.multiple_of(c * LANES, LANES)
        hi, lo = split(value.T)
        xt[0:channels, pl.ds(base, LANES)] = hi
        xt[channels : 2 * channels, pl.ds(base, LANES)] = lo

    def add_sums(value):
        sums[...] += value.reshape(LANES // 8, 8, channels).sum(0)

    def convert(c):
        at = pl.multiple_of(c * LANES, LANES)
        source = pl.multiple_of(at - halo, LANES)
        for r in range(2):
            xs[r, pl.ds(at + PAD, LANES), :] = raw[r, pl.ds(source, LANES), :].astype(F32)

    def plain(c, carry):
        convert(c)
        value = channelize(c)
        add_sums(value)
        store_columns(c, value)
        return carry

    def keep_power(c, value):
        power[pl.ds(pl.multiple_of(c * LANES, LANES), LANES), :] = value

    def shared(c, carry):
        convert(c)
        value = channelize(c)
        add_sums(value)
        store_columns(c, value)
        keep_power(c, value)
        return carry

    def opening(c, carry):
        convert(c)
        value = channelize(c)
        add_sums(value)
        keep_power(c, value)
        return carry

    def early(c, carry):
        keep_power(c, channelize(c))
        return carry

    sums[...] = jnp.zeros_like(sums)

    def width(k):
        return (blocks[k][1] - blocks[k][0]) * LANES + context

    def merge_local(k):
        end = blocks[k][1] * LANES
        begin = end - width(k)
        extra = min(LANES, begin)
        single = amat[...].astype(BF16)
        sorter = jnp.concatenate([single, single], axis=1)
        sorted_rows = dot(sorter, xt[:, begin - extra : end])
        acc = None
        for b in reversed(range(LSHIFT)):
            these = sorted_rows[ROW[b] : ROW[b + 1]]
            if acc is None:
                acc = these
                continue
            acc = pltpu.roll(acc, 1, 1)
            if these.shape[0] > acc.shape[0]:
                shared_rows = acc.shape[0]
                acc = jnp.concatenate([acc + these[:shared_rows], these[shared_rows:]], axis=0)
            else:
                acc = acc + these
        out = acc[(LLEVELS - 1) * TRIAL_DEV :]
        for a in reversed(range(LLEVELS - 1)):
            out = pltpu.roll(out, LSHIFT, 1) + acc[a * TRIAL_DEV : (a + 1) * TRIAL_DEV]
        series[0, :, offsets[k] : offsets[k] + width(k)] = out[:, extra:]

    def exchange(j, k):
        size = width(k) + (LANES if k == 0 else 0)
        where = pl.ds(offsets[k], size)
        return pltpu.make_async_remote_copy(
            src_ref=series.at[j, :, where], dst_ref=arrived.at[j, :, where],
            send_sem=x_send.at[j, k], recv_sem=x_recv.at[j, k],
            device_id={"freq": freq ^ (1 << j)}, device_id_type=MESH,
        )

    eye = lax.broadcasted_iota(jnp.int32, (TRIAL_DEV, TRIAL_DEV), 0) == lax.broadcasted_iota(
        jnp.int32, (TRIAL_DEV, TRIAL_DEV), 1
    )
    shift_cols = []
    for j in range(levels):
        shift_row = jnp.broadcast_to(xshift_ref[j : j + 1, :].astype(F32), (TRIAL_DEV, TRIAL_DEV))
        shift_cols.append(jnp.sum(jnp.where(eye, shift_row, 0.0), axis=1, keepdims=True).astype(jnp.int32))

    def merge_across(j, k):
        exchange(j, k).wait()
        here = slice(offsets[k], offsets[k] + width(k))
        upper = ((freq >> j) & 1) == 1
        mine, theirs = series[j, :, here], arrived[j, :, here]
        leading = jnp.where(upper, theirs, mine)
        trailing = jnp.where(upper, mine, theirs)
        for bit in range((TRIAL_DEV << j).bit_length() - 1):
            trailing = jnp.where(
                ((shift_cols[j] >> bit) & 1) == 1, pltpu.roll(trailing, 1 << bit, 1), trailing
            )
        merged = leading + trailing
        if k == 0:
            past = slice(here.stop, here.stop + LANES)
            totals = series[j, :, past] + arrived[j, :, past]
        if j + 1 < levels:
            series[j + 1, :, here] = merged
            if k == 0:
                series[j + 1, :, past] = totals
            exchange(j + 1, k).start()
        else:
            lo, hi = ((c - first) * LANES for c in blocks[k])
            final[:, lo:hi] = merged[:, context:]
            if k == 0:
                final[:, frames : frames + LANES] = totals

    ready = []

    def advance():
        moved = ready[:]
        ready.clear()
        for j, k in moved:
            merge_across(j, k)
            if j + 1 < levels:
                ready.append((j + 1, k))

    def take_tail():
        send_tail.wait()
        inside = (tm > 0).astype(F32)
        for r in range(2):
            xs[r, 0:PAD, :] = jnp.zeros((PAD, channels), F32)
            xs[r, PAD : PAD + halo, :] = tail[r].astype(F32) * inside

    late_tail = begin_pre > first
    copies[0].wait()
    if late_tail:
        convert(begin_pre - 1)
    else:
        take_tail()
    lax.fori_loop(begin_pre, blocks[1][0], shared, 0, unroll=2)
    for at, k in enumerate(order[:-1]):
        if at:
            copies[at].wait()
        lax.fori_loop(blocks[k][0], blocks[k][1], plain, 0, unroll=min(UNROLL, blocks[k][1] - blocks[k][0]))
        merge_local(k)
        exchange(0, k).start()
        advance()
        ready.append((0, k))

    if late_tail:
        if copies[-1] is not None:
            copies[-1].wait()
        take_tail()
        lax.fori_loop(first, begin_pre, opening, 0, unroll=True)
    psums[0] = sums[...]
    send_sums = pltpu.make_async_remote_copy(
        src_ref=psums.at[0], dst_ref=psums.at[1],
        send_sem=sum_sem.at[0], recv_sem=sum_sem.at[1], device_id=other, device_id_type=MESH,
    )
    send_sums.start()
    lax.fori_loop(0, first, early, 0)
    send_sums.wait()
    mean = jnp.sum(psums[0] + psums[1], axis=0, keepdims=True) * (1.0 / (frames * tm_size))

    def level0(c, carry):
        base = pl.multiple_of(c * LANES, LANES)
        keep = jnp.logical_or(c >= first, tm > 0).astype(F32)
        store_columns(c, (power[pl.ds(base, LANES), :] - mean) * keep)
        return carry

    lax.fori_loop(0, blocks[0][1], level0, 0, unroll=5 if blocks[0][1] % 5 == 0 else 1)
    merge_local(0)
    band_total = jnp.broadcast_to(jnp.sum(mean, axis=1, keepdims=True), (TRIAL_DEV, LANES))
    series[0, :, offsets[0] + width(0) : offsets[0] + width(0) + LANES] = band_total
    exchange(0, 0).start()
    advance()
    ready.append((0, 0))

    group = LANES // STRIDE
    templates = index_ref.shape[0]
    lane = lax.broadcasted_iota(jnp.int32, (WIN, LANES), 1)
    offset = lax.broadcasted_iota(jnp.int32, (WIN, index_ref.shape[1]), 0)

    def place(n, carry):
        hit = jnp.where(offset == index_ref[pl.ds(n, 1), :], weight_ref[pl.ds(n, 1), :], 0.0)
        column = jnp.sum(hit, axis=1, keepdims=True)
        toep[0:WIN, :] = jnp.where(lax.rem(lane, templates) == n, column, toep[0:WIN, :])
        return carry

    span = toep.shape[0]
    toep[...] = jnp.zeros_like(toep)
    steps = levels + 1
    done = 0
    while ready:
        upto = min(templates, done + -(-templates // steps))
        lax.fori_loop(done, upto, place, 0)
        done = upto
        advance()
    lax.fori_loop(done, templates, place, 0)
    base_rows = toep[0:WIN, :]
    placed = jnp.zeros((span, LANES), F32)
    for i in range(group):
        mine = jnp.where(lane // templates == i, base_rows, 0.0)
        placed = placed + jnp.concatenate(
            ([jnp.zeros((STRIDE * i, LANES), F32)] if i else [])
            + [mine, jnp.zeros((span - WIN - STRIDE * i, LANES), F32)], axis=0
        )
    toep_hi, toep_lo = split(placed)

    factor = 1.0 / math.sqrt(channels << levels)
    head[...] = final[:, 0:WIN] * factor
    send_head = pltpu.make_async_remote_copy(
        src_ref=head, dst_ref=nexthead,
        send_sem=head_sem.at[0], recv_sem=head_sem.at[1], device_id=other, device_id_type=MESH,
    )
    send_head.start()
    opened = (blocks[0][1] - first) * LANES
    total_mean = jnp.broadcast_to(final[:, frames : frames + 1], (TRIAL_DEV, frames - opened))
    dedispersed = jnp.concatenate([final[:, 0:opened], final[:, opened:frames] - total_mean], axis=1) * factor
    ded_ref[...] = dedispersed
    count = frames // LANES

    def correlate(wide, number):
        tiles = [wide[:, q * LANES : (q + 1) * LANES] for q in range(number + span // LANES - 1)]
        stacked = jnp.concatenate(
            [jnp.concatenate(tiles[u : u + number], axis=0) for u in range(span // LANES)], axis=1
        )
        hi, lo = split(stacked)
        return dot(hi, toep_hi) + dot(hi, toep_lo) + dot(lo, toep_hi)

    part = count - 4
    sco_ref[0 : part * TRIAL_DEV, :] = correlate(dedispersed, part)
    send_head.wait()
    follow = nexthead[...] * (tm < tm_size - 1).astype(F32)
    sco_ref[part * TRIAL_DEV :, :] = correlate(
        jnp.concatenate([dedispersed[:, part * LANES :], follow], axis=1), count - part
    )


def solution(mesh):
    freq_size, tm_size = mesh.shape["freq"], mesh.shape["tm"]
    levels = freq_size.bit_length() - 1
    reach = PFB_TAPS - 1 + LHALO + TRIAL_DEV * (freq_size - 1)
    halo = -(-reach // LANES) * LANES
    context = -(-TRIAL_DEV * (freq_size - 1) // LANES) * LANES

    def on_device(voltages, pfb_taps, local_shift, cross_shift, tap_index, tap_weight):
        frames, channels = voltages.shape[1:]
        templates = tap_index.shape[0]
        total = halo + frames
        span = WIN + LANES
        blocks = plan(frames, halo, context, reach)
        offsets, room = [], 0
        for k, (lo, hi) in enumerate(blocks):
            offsets.append(room)
            room += (hi - lo) * LANES + context + (LANES if k == 0 else 0)
        mask, spread = delay_tables(channels)
        vmem = pl.BlockSpec(memory_space=pltpu.VMEM)
        hbm = pl.BlockSpec(memory_space=pl.ANY)
        groups = frames // LANES
        dft = dft_tables(channels)
        dedispersed, scores = pl.pallas_call(
            functools.partial(kernel, (frames, halo, context, levels, channels, tm_size), blocks, offsets),
            out_shape=(
                jax.ShapeDtypeStruct((TRIAL_DEV, frames), F32),
                jax.ShapeDtypeStruct((groups * TRIAL_DEV, LANES), F32),
            ),
            in_specs=[hbm] + [vmem] * 5 + [hbm] * 3,
            out_specs=(vmem, vmem),
            scratch_shapes=[
                pltpu.VMEM((2, frames, channels), BF16),
                pltpu.VMEM((2, halo, channels), BF16),
                pltpu.VMEM((2, PAD + total, channels), F32),
                pltpu.VMEM((blocks[0][1] * LANES, channels), F32),
                pltpu.VMEM((8, channels), F32),
                pltpu.VMEM((2, 8, channels), F32),
                pltpu.VMEM((ROW[-1], channels), F32),
                pltpu.VMEM((2 * channels, total), BF16),
                pltpu.VMEM((levels, TRIAL_DEV, room), F32),
                pltpu.VMEM((levels, TRIAL_DEV, room), F32),
                pltpu.VMEM((TRIAL_DEV, frames + LANES), F32),
                pltpu.VMEM((TRIAL_DEV, WIN), F32),
                pltpu.VMEM((TRIAL_DEV, WIN), F32),
                pltpu.VMEM((span, LANES), F32),
                pltpu.VMEM(dft.shape, BF16),
                pltpu.VMEM(mask.shape, F32),
                pltpu.VMEM(spread.shape, BF16),
                pltpu.SemaphoreType.DMA((len(blocks),)),
                pltpu.SemaphoreType.DMA((3,)),
                pltpu.SemaphoreType.DMA((2,)),
                pltpu.SemaphoreType.DMA((2,)),
                pltpu.SemaphoreType.DMA((levels, len(blocks))),
                pltpu.SemaphoreType.DMA((levels, len(blocks))),
                pltpu.SemaphoreType.DMA((2,)),
            ],
            compiler_params=pltpu.CompilerParams(collective_id=0, has_side_effects=True),
        )(
            voltages, pfb_taps, local_shift, cross_shift, tap_index, tap_weight,
            jnp.asarray(dft), jnp.asarray(mask), jnp.asarray(spread),
        )
        placed = scores.reshape(groups, TRIAL_DEV, LANES // STRIDE, templates)
        placed = placed.transpose(1, 3, 0, 2).reshape(TRIAL_DEV, templates, frames // STRIDE)
        return dedispersed, placed

    return jax.shard_map(
        on_device,
        mesh=mesh,
        in_specs=(P("beam", "tm", "freq"), P(), P(None, "freq"), P(None, "freq"), P(), P()),
        out_specs=(P(("beam", "freq"), "tm"), P(("beam", "freq"), None, "tm")),
        check_vma=False,
    )
```
